32 devices in a mesh: region: 4 (over z), tok: 8 (over y, x, core).
Axes of the slice: x: 2, y: 2, z: 4, core: 2. Of those that a mesh axis runs over, the one named last changes fastest.
Arguments:
- tokens: bfloat16 [4096, 1024], P(('region', 'tok')), may hold values from -6 to 6
- w_query: bfloat16 [1024, 1024], P('tok'), may hold values from -0.1875 to 0.1875
- w_key: bfloat16 [1024, 1024], P('tok'), may hold values from -0.1875 to 0.1875
- w_value: bfloat16 [1024, 1024], P('tok'), may hold values from -0.1875 to 0.1875
- w_out: bfloat16 [1024, 1024], P(None, 'tok'), may hold values from -0.1875 to 0.1875
- past_keys: bfloat16 [4, 4096, 1024], P(None, ('region', 'tok')), may hold values from -600 to 600
- past_values: bfloat16 [4, 4096, 1024], P(None, ('region', 'tok')), may hold values from -6 to 6
- nb_block: int32 [32, 8], replicated, may hold values from 0 to 31, as said below
- nb_frame: int32 [32, 8], replicated, may hold values from 0 to 3, as said below
- nb_count: int32 [32], replicated, may hold values from 2 to 8
- block_slot: int32 [32], replicated, may hold values from 0 to 31, as said below
Outputs:
- attn_out: bfloat16 [4096, 1024], P(('region', 'tok'))
The draws below stay inside these ranges and needn't reach their ends.
Inputs may be any that keep to these rules, and one draw needn't show every extreme that they name: block_slot is a permutation of the block ids; device i of region+tok stores slot i (one block per device). `nb_block`: the entries of one query block name distinct blocks. For the query blocks of device (r, c) of region+tok, entry 0 names one and the same block and frame stored in region group r - 1, entry 1 one and the same stored in group r + 1 (periodic), the other entries blocks stored in group r, on tok indices other than those of entries 0 and 1. For each group r and tok index t, exactly one device of group r reads its entry 0 from tok index t of group r - 1, and exactly one reads its entry 1 from tok index t of group r + 1. All entries of query blocks of devices with tok index c that name blocks stored on one device name one and the same block and frame. `nb_frame`: see nb_block.
All inputs are finite; a program needn't handle non-finite values.
Results may differ from the reference program's by a relative error of at most 0.0035.
The reference program's roundings to bfloat16 on the way count: a program that leaves them out, or rounds other values in their place, can miss the bound.
Values may be sent and summed in bfloat16 or wider, within the bound.
No kernel may reach another device: no remote copies, remote signals or barrier semaphores. Data moves between devices by JAX's collectives and lax.ppermute only.
A program may use at most 128 MiB of HBM per device.

```python
import math
import jax
import jax.numpy as jnp
from jax import lax

D = 1024
HEADS = 8
HEAD_DIM = 128
QB = 128
FRAMES = 4
MAXNB = 8
BLK_DEV = 1
TOKENS = 4096
NBLK = 32
N_REGION = 4
N_TOK = 8


def build_lists(key):
    n_devices = N_REGION * N_TOK
    n_pieces = BLK_DEV * FRAMES
    base_key = jax.random.fold_in(key, 7)
    key_perm, key_offer, key_cycle, key_own, key_count = jax.random.split(base_key, 5)
    slot_perm = jax.random.permutation(key_perm, NBLK).astype(jnp.int32)
    inverse = jnp.zeros((NBLK,), jnp.int32).at[slot_perm].set(jnp.arange(NBLK, dtype=jnp.int32))
    offer_table = jax.random.randint(key_offer, (N_REGION, N_TOK, N_TOK), 0, n_pieces).astype(jnp.int32)
    cycles = jax.vmap(lambda one_key: jax.random.permutation(one_key, N_TOK))(jax.random.split(key_cycle, N_REGION)).astype(jnp.int32)
    region_rows = jnp.broadcast_to(jnp.arange(N_REGION, dtype=jnp.int32)[:, None], (N_REGION, N_TOK))
    place_values = jnp.broadcast_to(jnp.arange(N_TOK, dtype=jnp.int32)[None, :], (N_REGION, N_TOK))
    places = jnp.zeros((N_REGION, N_TOK), jnp.int32).at[region_rows, cycles].set(place_values)
    device_ids = jnp.arange(n_devices, dtype=jnp.int32)
    dev_region = device_ids // N_TOK
    dev_tok = device_ids % N_TOK
    dev_place = places[dev_region, dev_tok]
    lower_tok = cycles[dev_region, (dev_place + 1) % N_TOK]
    upper_tok = cycles[dev_region, (dev_place + 2) % N_TOK]
    own_pick = jax.vmap(lambda one_key: jax.random.permutation(one_key, N_TOK - 2))(jax.random.split(key_own, NBLK))
    own_pick = own_pick[:, :MAXNB - 2].astype(jnp.int32).reshape(n_devices, BLK_DEV, MAXNB - 2)
    own_tok = cycles[dev_region[:, None, None], (dev_place[:, None, None] + 3 + own_pick) % N_TOK]
    lower_col = jnp.broadcast_to(lower_tok[:, None, None], (n_devices, BLK_DEV, 1))
    upper_col = jnp.broadcast_to(upper_tok[:, None, None], (n_devices, BLK_DEV, 1))
    source_tok = jnp.concatenate([lower_col, upper_col, own_tok], 2)
    lower_reg = jnp.broadcast_to(((dev_region - 1) % N_REGION)[:, None, None], (n_devices, BLK_DEV, 1))
    upper_reg = jnp.broadcast_to(((dev_region + 1) % N_REGION)[:, None, None], (n_devices, BLK_DEV, 1))
    same_reg = jnp.broadcast_to(dev_region[:, None, None], (n_devices, BLK_DEV, MAXNB - 2))
    source_reg = jnp.concatenate([lower_reg, upper_reg, same_reg], 2)
    dest_tok = jnp.broadcast_to(dev_tok[:, None, None], (n_devices, BLK_DEV, MAXNB))
    piece_ids = offer_table[source_reg, source_tok, dest_tok]
    slot_ids = (source_reg * N_TOK + source_tok) * BLK_DEV + piece_ids // FRAMES
    block_ids = inverse[slot_ids].reshape(NBLK, MAXNB)
    frame_ids = (piece_ids % FRAMES).reshape(NBLK, MAXNB)
    counts = jax.random.randint(key_count, (NBLK,), 2, MAXNB + 1).astype(jnp.int32)
    counts = counts.at[0].set(MAXNB).at[1].set(2)
    return (slot_perm, block_ids, frame_ids, counts)


def draw_block_slot(key, part):
    return build_lists(key)[0]


def draw_nb_block(key, part):
    return build_lists(key)[1]


def draw_nb_frame(key, part):
    return build_lists(key)[2]


def draw_nb_count(key, part):
    return build_lists(key)[3]


def draw_past_keys(key, part):
    key_base, key_piece, key_factor = jax.random.split(jax.random.fold_in(key, 11), 3)
    base_draw = jax.random.truncated_normal(key_base, -6.0, 6.0, (FRAMES, TOKENS, D), jnp.float32)
    scale_low = 10.0
    scale_high = 90.0
    marked = jax.random.randint(key_piece, (FRAMES, NBLK, 1), 0, 32) == 0
    row_factor = jnp.exp(jax.random.uniform(key_factor, (FRAMES, NBLK, QB), jnp.float32, math.log(scale_low), math.log(scale_high)))
    factor = jnp.where(marked, row_factor, jnp.float32(1.0)).reshape(FRAMES, TOKENS, 1)
    return (base_draw * factor).astype(jnp.bfloat16)


def block_levels(stream_key, extent, cuts, low, high):
    def one(position, parts):
        draws = jax.random.uniform(jax.random.fold_in(jax.random.fold_in(stream_key, 6), position), (parts,), jnp.float32, low / len(cuts), high / len(cuts))
        return jnp.repeat(jnp.exp(draws), extent[position] // parts).reshape((-1,) + (1,) * (len(extent) - position - 1))

    factor_of = one(*cuts[0])
    for cut in cuts[1:]:
        factor_of = factor_of * one(*cut)
    return factor_of


def gaussian(rng, extent, scale, most, cuts=(), held_as=jnp.bfloat16):
    entries = jax.random.normal(rng, extent, jnp.float32) * scale
    if len(cuts) > 0:
        entries = block_levels(rng, extent, cuts, -0.22, 0.18) * entries
    return jnp.clip(entries, min=-most, max=most).astype(held_as)


def setup_inputs(seed: int = 0) -> dict:
    keys = jax.random.split(jax.random.key(seed), 12)
    return {
        "tokens": gaussian(keys[0], (TOKENS, D), 1.0, 6.0, ((0, 32),)),
        "w_query": gaussian(keys[1], (D, D), D ** -0.5, 0.1875, ((0, 8),)),
        "w_key": gaussian(keys[2], (D, D), D ** -0.5, 0.1875, ((0, 8),)),
        "w_value": gaussian(keys[3], (D, D), D ** -0.5, 0.1875, ((0, 8),)),
        "w_out": gaussian(keys[4], (D, D), D ** -0.5, 0.1875, ((1, 8),)),
        "past_keys": draw_past_keys(jax.random.fold_in(keys[11], 71), 0),
        "past_values": gaussian(keys[6], (FRAMES, TOKENS, D), 1.0, 6.0, ((1, 32),)),
        "nb_block": draw_nb_block(jax.random.fold_in(keys[11], 71), 0),
        "nb_frame": draw_nb_frame(jax.random.fold_in(keys[11], 71), 0),
        "nb_count": draw_nb_count(jax.random.fold_in(keys[11], 71), 0),
        "block_slot": draw_block_slot(jax.random.fold_in(keys[11], 71), 0),
    }


def reference(tokens, w_query, w_key, w_value, w_out, past_keys, past_values, nb_block, nb_frame, nb_count, block_slot):
    queries = jnp.dot(tokens, w_query, preferred_element_type=jnp.float32).astype(jnp.bfloat16)
    keys_new = jnp.dot(tokens, w_key, preferred_element_type=jnp.float32).astype(jnp.bfloat16)
    values_new = jnp.dot(tokens, w_value, preferred_element_type=jnp.float32).astype(jnp.bfloat16)
    key_cache = past_keys.reshape(FRAMES, NBLK, QB, D)
    value_cache = past_values.reshape(FRAMES, NBLK, QB, D)
    slot_table = jnp.take(block_slot, nb_block, axis=0)
    attn_scale = HEAD_DIM ** -0.5

    def one_block(block_id):
        query_rows = lax.dynamic_slice_in_dim(queries, block_id * QB, QB, 0)
        own_keys = lax.dynamic_slice_in_dim(keys_new, block_id * QB, QB, 0)
        own_values = lax.dynamic_slice_in_dim(values_new, block_id * QB, QB, 0)
        frame_list = nb_frame[block_id]
        slot_list = slot_table[block_id]
        far_keys = key_cache[frame_list, slot_list]
        far_values = value_cache[frame_list, slot_list]
        key_list = jnp.concatenate([own_keys[None], far_keys], 0).reshape((1 + MAXNB) * QB, HEADS, HEAD_DIM)
        value_list = jnp.concatenate([own_values[None], far_values], 0).reshape((1 + MAXNB) * QB, HEADS, HEAD_DIM)
        query_heads = query_rows.reshape(QB, HEADS, HEAD_DIM)
        scores = jnp.einsum("qhd,khd->hqk", query_heads.astype(jnp.float32), key_list.astype(jnp.float32)) * attn_scale
        entry_live = jnp.arange(MAXNB, dtype=jnp.int32) < nb_count[block_id]
        live_mask = jnp.concatenate([jnp.ones((QB,), bool), jnp.repeat(entry_live, QB)], 0)
        scores = jnp.where(live_mask[None, None, :], scores, jnp.float32(-1e30))
        row_max = jnp.max(scores, axis=-1, keepdims=True)
        exp_weights = jnp.where(live_mask[None, None, :], jnp.exp(scores - row_max), jnp.float32(0.0))
        row_total = jnp.sum(exp_weights, axis=-1)
        prob_bf = exp_weights.astype(jnp.bfloat16)
        context = jnp.einsum("hqk,khd->qhd", prob_bf.astype(jnp.float32), value_list.astype(jnp.float32))
        context = context / jnp.transpose(row_total)[:, :, None]
        return context.reshape(QB, D).astype(jnp.bfloat16)

    context_all = lax.map(one_block, jnp.arange(NBLK, dtype=jnp.int32)).reshape(TOKENS, D)
    return jnp.dot(context_all, w_out, preferred_element_type=jnp.float32).astype(jnp.bfloat16)
```

```python
import jax
import jax.numpy as jnp
from jax import lax
from jax.experimental import pallas as pl
from jax.experimental.pallas import tpu as pltpu
from jax.sharding import PartitionSpec as P

HEADS = 8
QB = 128


ANY = pl.BlockSpec(memory_space=pl.ANY)
VMEM = pl.BlockSpec(memory_space=pltpu.VMEM)
SMEM = pl.BlockSpec(memory_space=pltpu.SMEM)


def shifted(block, axis, distance):
    devices = range(lax.axis_size(axis))
    route = [((i - distance) % len(devices), i) for i in devices]
    return lax.ppermute(block, axis, route)


def partner(block, mask):
    route = [(i, i ^ mask) for i in range(lax.axis_size("tok"))]
    return lax.ppermute(block, "tok", route)


def cost(flops, moved):
    return pl.CostEstimate(flops=flops, bytes_accessed=moved, transcendentals=0)


def gathered(shard):
    n_tok = lax.axis_size("tok")
    even = {0: shard}
    for mask in range(2, n_tok, 2):
        even[mask] = partner(shard, mask)
    return [even[m] if m % 2 == 0 else partner(even[m - 1], 1) for m in range(n_tok)]


def exchanged(pieces):
    return [pieces[0]] + [partner(pieces[m], m) for m in range(1, len(pieces))]


def pack_cache(cache, n_tok):
    frames, rows, width = cache.shape
    head_size = width // n_tok

    def body(cache_ref, *out_refs):
        tok_id = lax.axis_index("tok")
        for m in range(n_tok):
            start = pl.multiple_of((tok_id ^ m) * head_size, head_size)
            out_refs[m][...] = cache_ref[:, :, pl.ds(start, head_size)]

    piece = jax.ShapeDtypeStruct((frames, rows, head_size), cache.dtype)
    return pl.pallas_call(
        body,
        out_shape=[piece] * n_tok,
        in_specs=[VMEM],
        out_specs=[VMEM] * n_tok,
        name="pack_cache",
        cost_estimate=cost(0, 2 * cache.size * 2),
    )(cache)


def pack_weights(weights, n_tok):
    rows, width = weights[0].shape
    head_size = width // n_tok
    n_weights = len(weights)

    def body(*refs):
        tok_id = lax.axis_index("tok")
        for m in range(n_tok):
            start = pl.multiple_of((tok_id ^ m) * head_size, head_size)
            for j in range(n_weights):
                refs[n_weights + m][:, j * head_size : (j + 1) * head_size] = refs[j][
                    :, pl.ds(start, head_size)
                ]

    piece = jax.ShapeDtypeStruct((rows, n_weights * head_size), weights[0].dtype)
    return pl.pallas_call(
        body,
        out_shape=[piece] * n_tok,
        in_specs=[VMEM] * n_weights,
        out_specs=[VMEM] * n_tok,
        name="pack_weights",
        cost_estimate=cost(0, 2 * n_weights * rows * width * 2),
    )(*weights)


def pick_sides(pieces, tables, n_region, n_tok):
    frames, rows, head_size = pieces[0].shape

    def body(block_ref, frame_ref, slot_ref, *refs):
        piece_refs = refs[:n_tok]
        up_ref, down_ref, held, sems = refs[n_tok:]
        copies = [
            pltpu.make_async_copy(piece_refs[m], held.at[m], sems.at[m]) for m in range(n_tok)
        ]
        for copy in copies:
            copy.start()
        region_id = lax.axis_index("region")
        tok_id = lax.axis_index("tok")
        upper = lax.rem(region_id + 1, n_region)
        lower = lax.rem(region_id + n_region - 1, n_region)
        for copy in copies:
            copy.wait()
        for entry, reader, out_ref in ((0, upper, up_ref), (1, lower, down_ref)):
            for m in range(n_tok):
                query_block = reader * n_tok + (tok_id ^ m)
                slot = slot_ref[block_ref[entry, query_block]]
                source = lax.rem(slot, n_tok) ^ tok_id
                out_ref[m] = held[source, frame_ref[entry, query_block]]

    side = jax.ShapeDtypeStruct((n_tok, rows, head_size), pieces[0].dtype)
    return pl.pallas_call(
        body,
        out_shape=[side, side],
        in_specs=[SMEM] * 3 + [ANY] * n_tok,
        out_specs=[VMEM] * 2,
        scratch_shapes=[
            pltpu.VMEM((n_tok, frames, rows, head_size), pieces[0].dtype),
            pltpu.SemaphoreType.DMA((n_tok,)),
        ],
        name="pick_sides",
        cost_estimate=cost(0, 2 * n_tok * (frames + 2) * rows * head_size),
    )(*tables, *pieces)


def project(token_blocks, weight_rows):
    n_tok = len(token_blocks)
    rows, width = token_blocks[0].shape
    depth, columns = weight_rows[0].shape

    def body(*refs):
        token_refs = refs[:n_tok]
        weight_refs = refs[n_tok : 2 * n_tok]
        out_ref, whole, held, sems = refs[2 * n_tok :]
        tok_id = lax.axis_index("tok")
        copies = []
        for m in range(n_tok):
            start = pl.multiple_of((tok_id ^ m) * depth, depth)
            copies.append(
                pltpu.make_async_copy(
                    weight_refs[m], whole.at[pl.ds(start, depth), :], sems.at[m]
                )
            )
            copies.append(
                pltpu.make_async_copy(token_refs[m], held.at[m], sems.at[n_tok + m])
            )
        for copy in copies:
            copy.start()
        for copy in copies:
            copy.wait()
        for m in range(n_tok):
            out_ref[m] = jnp.dot(
                held[m], whole[...], preferred_element_type=jnp.float32
            ).astype(out_ref.dtype)

    return pl.pallas_call(
        body,
        out_shape=jax.ShapeDtypeStruct((n_tok, rows, columns), token_blocks[0].dtype),
        in_specs=[ANY] * (2 * n_tok),
        out_specs=VMEM,
        scratch_shapes=[
            pltpu.VMEM((n_tok * depth, columns), token_blocks[0].dtype),
            pltpu.VMEM((n_tok, rows, width), token_blocks[0].dtype),
            pltpu.SemaphoreType.DMA((2 * n_tok,)),
        ],
        name="project",
        cost_estimate=cost(
            2 * n_tok * rows * width * columns, 2 * n_tok * (rows * width + depth * columns)
        ),
    )(*token_blocks, *weight_rows)


def attend(projected, keys, values, side_keys, side_values, tables, counts):
    n_tok, rows, columns = projected.shape
    head_size = columns // 3
    frames = keys[0].shape[0]
    max_entries = tables[0].shape[0]
    scale = head_size ** (-0.5)
    across = (((1,), (1,)), ((), ()))

    def body(block_ref, frame_ref, slot_ref, count_ref, *refs):
        proj_ref = refs[0]
        key_refs = refs[1 : 1 + n_tok]
        value_refs = refs[1 + n_tok : 1 + 2 * n_tok]
        side_refs = refs[1 + 2 * n_tok : 5 + 2 * n_tok]
        out_refs = refs[5 + 2 * n_tok : 5 + 3 * n_tok]
        held_keys, held_values, sems = refs[5 + 3 * n_tok :]
        copies = []
        for m in range(n_tok):
            copies.append(pltpu.make_async_copy(key_refs[m], held_keys.at[m], sems.at[m]))
            copies.append(
                pltpu.make_async_copy(value_refs[m], held_values.at[m], sems.at[n_tok + m])
            )
        for copy in copies:
            copy.start()
        region_id = lax.axis_index("region")
        tok_id = lax.axis_index("tok")
        for copy in copies:
            copy.wait()
        for m in range(n_tok):
            query_block = region_id * n_tok + (tok_id ^ m)
            live = count_ref[query_block]
            query = proj_ref[m, :, :head_size]
            key_list = [proj_ref[m, :, head_size : 2 * head_size]]
            value_list = [proj_ref[m, :, 2 * head_size :]]
            for entry in range(2):
                key_list.append(side_refs[entry][m])
                value_list.append(side_refs[2 + entry][m])
            for entry in range(2, max_entries):
                slot = slot_ref[block_ref[entry, query_block]]
                source = lax.rem(slot, n_tok) ^ tok_id
                frame = frame_ref[entry, query_block]
                key_list.append(held_keys[source, frame])
                value_list.append(held_values[source, frame])
            scores = (
                lax.dot_general(
                    query,
                    jnp.concatenate(key_list, 0),
                    across,
                    preferred_element_type=jnp.float32,
                )
                * scale
            )
            column = lax.broadcasted_iota(jnp.int32, scores.shape, 1)
            scores = jnp.where(column < (live + 1) * rows, scores, jnp.float32(-1e30))
            row_max = jnp.max(scores, axis=1, keepdims=True)
            weights = jnp.exp(scores - row_max)
            total = jnp.sum(weights, axis=1, keepdims=True)
            context = jnp.dot(
                weights.astype(jnp.bfloat16),
                jnp.concatenate(value_list, 0),
                preferred_element_type=jnp.float32,
            )
            out_refs[m][...] = (context / total).astype(out_refs[m].dtype)

    block = jax.ShapeDtypeStruct((rows, head_size), projected.dtype)
    cached = (n_tok, frames, rows, head_size)
    return pl.pallas_call(
        body,
        out_shape=[block] * n_tok,
        in_specs=[SMEM] * 4 + [VMEM] + [ANY] * (2 * n_tok) + [VMEM] * 4,
        out_specs=[VMEM] * n_tok,
        scratch_shapes=[
            pltpu.VMEM(cached, projected.dtype),
            pltpu.VMEM(cached, projected.dtype),
            pltpu.SemaphoreType.DMA((2 * n_tok,)),
        ],
        name="attend",
        cost_estimate=cost(
            4 * n_tok * rows * rows * (max_entries + 1) * head_size,
            4 * n_tok * frames * rows * head_size,
        ),
    )(*tables, counts, projected, *keys, *values, *side_keys, *side_values)


def mix(context_heads, out_columns):
    n_tok = len(context_heads)
    rows, head_size = context_heads[0].shape
    width, columns = out_columns[0].shape

    def body(*refs):
        context_refs = refs[:n_tok]
        column_refs = refs[n_tok : 2 * n_tok]
        out_ref, context, whole, sems = refs[2 * n_tok :]
        tok_id = lax.axis_index("tok")
        copies = []
        for m in range(n_tok):
            start = pl.multiple_of((tok_id ^ m) * head_size, head_size)
            copies.append(
                pltpu.make_async_copy(
                    context_refs[m], context.at[:, pl.ds(start, head_size)], sems.at[m]
                )
            )
            start = pl.multiple_of((tok_id ^ m) * columns, columns)
            copies.append(
                pltpu.make_async_copy(
                    column_refs[m], whole.at[:, pl.ds(start, columns)], sems.at[n_tok + m]
                )
            )
        for copy in copies:
            copy.start()
        for copy in copies:
            copy.wait()
        out_ref[...] = jnp.dot(
            context[...], whole[...], preferred_element_type=jnp.float32
        ).astype(out_ref.dtype)

    dtype = context_heads[0].dtype
    return pl.pallas_call(
        body,
        out_shape=jax.ShapeDtypeStruct((rows, n_tok * columns), dtype),
        in_specs=[ANY] * (2 * n_tok),
        out_specs=VMEM,
        scratch_shapes=[
            pltpu.VMEM((rows, n_tok * head_size), dtype),
            pltpu.VMEM((width, n_tok * columns), dtype),
            pltpu.SemaphoreType.DMA((2 * n_tok,)),
        ],
        name="mix",
        cost_estimate=cost(
            2 * rows * width * n_tok * columns, 2 * width * n_tok * columns
        ),
    )(*context_heads, *out_columns)


def head_per_device(
    tokens,
    w_query,
    w_key,
    w_value,
    w_out,
    past_keys,
    past_values,
    nb_block,
    nb_frame,
    nb_count,
    block_slot,
):
    n_region = lax.axis_size("region")
    n_tok = lax.axis_size("tok")
    tables = (nb_block.T, nb_frame.T, block_slot)
    keys = exchanged(pack_cache(past_keys, n_tok))
    values = exchanged(pack_cache(past_values, n_tok))
    up_keys, down_keys = pick_sides(keys, tables, n_region, n_tok)
    below_keys, above_keys = shifted(up_keys, "region", 1), shifted(down_keys, "region", -1)
    up_values, down_values = pick_sides(values, tables, n_region, n_tok)
    below_values = shifted(up_values, "region", 1)
    above_values = shifted(down_values, "region", -1)
    weight_rows = exchanged(pack_weights((w_query, w_key, w_value), n_tok))
    token_blocks = gathered(tokens)
    out_columns = gathered(w_out)
    projected = project(token_blocks, weight_rows)
    context = attend(
        projected,
        keys,
        values,
        (below_keys, above_keys),
        (below_values, above_values),
        tables,
        nb_count,
    )
    return mix(exchanged(context), out_columns)


def per_device(
    tokens,
    w_query,
    w_key,
    w_value,
    w_out,
    past_keys,
    past_values,
    nb_block,
    nb_frame,
    nb_count,
    block_slot,
):
    n_region = lax.axis_size("region")
    n_tok = lax.axis_size("tok")
    region_id = lax.axis_index("region")
    tok_id = lax.axis_index("tok")
    n_devices = n_region * n_tok
    my_device = region_id * n_tok + tok_id
    tok_rows, model_width = tokens.shape
    blocks_dev = tok_rows // QB
    n_blocks, max_entries = nb_block.shape
    head_size = model_width // HEADS
    whole_query, whole_key, whole_value = (
        lax.all_gather(w_query, "tok", axis=0, tiled=True),
        lax.all_gather(w_key, "tok", axis=0, tiled=True),
        lax.all_gather(w_value, "tok", axis=0, tiled=True),
    )
    proj_query = jnp.dot(tokens, whole_query, preferred_element_type=jnp.float32)
    proj_key = jnp.dot(tokens, whole_key, preferred_element_type=jnp.float32)
    proj_value = jnp.dot(tokens, whole_value, preferred_element_type=jnp.float32)
    queries = proj_query.astype(jnp.bfloat16)
    keys_new = proj_key.astype(jnp.bfloat16)
    values_new = proj_value.astype(jnp.bfloat16)
    slot_table = jnp.take(block_slot, nb_block, axis=0)
    source_dev = slot_table // blocks_dev
    source_tok = source_dev % n_tok
    flat_table = nb_frame * blocks_dev + slot_table % blocks_dev
    live_table = jnp.arange(max_entries, dtype=jnp.int32)[None, :] < nb_count[:, None]
    dest_tok = jnp.arange(n_blocks, dtype=jnp.int32) // blocks_dev % n_tok
    tok_range = jnp.arange(n_tok, dtype=jnp.int32)
    mine_flat = (live_table & (source_dev == my_device)).reshape(-1)
    dest_flat = jnp.broadcast_to(dest_tok[:, None], (n_blocks, max_entries)).reshape(-1)
    matches = mine_flat[None, :] & (dest_flat[None, :] == tok_range[:, None])
    offer_index = jnp.max(jnp.where(matches, flat_table.reshape(-1)[None, :], 0), axis=1)
    offer_keys = jnp.take(past_keys, offer_index, axis=0)
    offer_values = jnp.take(past_values, offer_index, axis=0)
    lead_tok = source_tok.reshape(n_devices, blocks_dev, max_entries)[:, 0, :2]
    lower_region = (region_id + n_region - 1) % n_region
    upper_region = (region_id + 1) % n_region
    my_start = my_device * blocks_dev
    my_tok_table = lax.dynamic_slice_in_dim(source_tok, my_start, blocks_dev, 0)
    got_keys, got_values = (
        lax.all_to_all(offer_keys, "tok", split_axis=0, concat_axis=0, tiled=True),
        lax.all_to_all(offer_values, "tok", split_axis=0, concat_axis=0, tiled=True),
    )
    upward_index = lax.dynamic_index_in_dim(
        lead_tok[:, 0], upper_region * n_tok + tok_id, 0, keepdims=False
    )
    downward_index = lax.dynamic_index_in_dim(
        lead_tok[:, 1], lower_region * n_tok + tok_id, 0, keepdims=False
    )
    upward_pair = jnp.concatenate(
        [
            lax.dynamic_slice_in_dim(got_keys, upward_index, 1, 0),
            lax.dynamic_slice_in_dim(got_values, upward_index, 1, 0),
        ],
        0,
    )
    downward_pair = jnp.concatenate(
        [
            lax.dynamic_slice_in_dim(got_keys, downward_index, 1, 0),
            lax.dynamic_slice_in_dim(got_values, downward_index, 1, 0),
        ],
        0,
    )
    below_pair = shifted(upward_pair, "region", 1)
    above_pair = shifted(downward_pair, "region", -1)
    own_index = my_tok_table[:, 2:].reshape(-1)
    own_keys = jnp.take(got_keys, own_index, axis=0).reshape(
        blocks_dev, (max_entries - 2) * QB, model_width
    )
    own_values = jnp.take(got_values, own_index, axis=0).reshape(
        blocks_dev, (max_entries - 2) * QB, model_width
    )
    side_keys = jnp.concatenate([below_pair[0], above_pair[0]], 0)[None]
    side_values = jnp.concatenate([below_pair[1], above_pair[1]], 0)[None]
    far_keys = jnp.concatenate([side_keys, own_keys], 1)
    far_values = jnp.concatenate([side_values, own_values], 1)
    key_list = jnp.concatenate([keys_new.reshape(blocks_dev, QB, model_width), far_keys], 1)
    value_list = jnp.concatenate([values_new.reshape(blocks_dev, QB, model_width), far_values], 1)
    list_len = key_list.shape[1]
    query_heads = queries.reshape(blocks_dev, QB, HEADS, head_size)
    key_heads = key_list.reshape(blocks_dev, list_len, HEADS, head_size)
    value_heads = value_list.reshape(blocks_dev, list_len, HEADS, head_size)
    attn_scale = head_size ** (-0.5)
    scores = (
        jnp.einsum("bqhd,bkhd->bhqk", query_heads, key_heads, preferred_element_type=jnp.float32)
        * attn_scale
    )
    my_counts = lax.dynamic_slice_in_dim(nb_count, my_start, blocks_dev, 0)
    entry_live = jnp.arange(max_entries, dtype=jnp.int32)[None, :] < my_counts[:, None]
    live_mask = jnp.concatenate(
        [jnp.ones((blocks_dev, QB), bool), jnp.repeat(entry_live, QB, axis=1)], 1
    )
    scores = jnp.where(live_mask[:, None, None, :], scores, jnp.float32(-1e30))
    row_max = jnp.max(scores, axis=-1, keepdims=True)
    exp_weights = jnp.where(
        live_mask[:, None, None, :], jnp.exp(scores - row_max), jnp.float32(0.0)
    )
    row_total = jnp.sum(exp_weights, axis=-1)
    prob_bf = exp_weights.astype(jnp.bfloat16)
    context = jnp.einsum(
        "bhqk,bkhd->bqhd", prob_bf, value_heads, preferred_element_type=jnp.float32
    )
    context = context / jnp.swapaxes(row_total, 1, 2)[:, :, :, None]
    context_bf = context.reshape(tok_rows, model_width).astype(jnp.bfloat16)
    whole_out = lax.all_gather(w_out, "tok", axis=1, tiled=True)
    mixed_out = jnp.dot(context_bf, whole_out, preferred_element_type=jnp.float32)
    return mixed_out.astype(jnp.bfloat16)


def solution(mesh):
    n_tok = mesh.shape["tok"]
    step = head_per_device if n_tok == HEADS else per_device
    return jax.shard_map(
        step,
        mesh=mesh,
        in_specs=(
            P(("region", "tok"), None),
            P("tok", None),
            P("tok", None),
            P("tok", None),
            P(None, "tok"),
            P(None, ("region", "tok"), None),
            P(None, ("region", "tok"), None),
            P(),
            P(),
            P(),
            P(),
        ),
        out_specs=P(("region", "tok"), None),
        check_vma=False,
    )
```

```python
import jax
import jax.numpy as jnp
from jax import lax
from jax.experimental import pallas as pl
from jax.experimental.pallas import tpu as pltpu
from jax.sharding import PartitionSpec as P

HEADS = 8
QB = 128


ANY = pl.BlockSpec(memory_space=pl.ANY)
VMEM = pl.BlockSpec(memory_space=pltpu.VMEM)
SMEM = pl.BlockSpec(memory_space=pltpu.SMEM)


def shifted(block, axis, distance):
    devices = range(lax.axis_size(axis))
    route = [((i - distance) % len(devices), i) for i in devices]
    return lax.ppermute(block, axis, route)


def partner(block, mask):
    route = [(i, i ^ mask) for i in range(lax.axis_size("tok"))]
    return lax.ppermute(block, "tok", route)


def gathered(shard):
    shards = [shard]
    for mask in range(1, lax.axis_size("tok")):
        near = mask % 2 == 1
        shards.append(partner(shards[mask - 1] if near else shard, 1 if near else mask))
    return shards


def exchanged(pieces):
    return [pieces[0]] + [partner(pieces[m], m) for m in range(1, len(pieces))]


def swapped(pieces):
    return lax.all_to_all(pieces, "tok", split_axis=0, concat_axis=0, tiled=True)


def kernel(body, arguments, out_shape, in_specs, out_specs, scratch, limit, flops, moved):
    return pl.pallas_call(
        body,
        out_shape=out_shape,
        in_specs=in_specs,
        out_specs=out_specs,
        scratch_shapes=scratch,
        compiler_params=pltpu.CompilerParams(vmem_limit_bytes=limit * 2**20),
        cost_estimate=pl.CostEstimate(flops=flops, bytes_accessed=moved, transcendentals=0),
    )(*arguments)


def pack(sources, n_tok, mirrored):
    width = sources[0].shape[-1]
    head_size = width // n_tok
    n_sources = len(sources)
    shape = sources[0].shape[:-1] + (n_sources * head_size,)
    dtype = sources[0].dtype

    def body(*refs):
        source_refs = refs[:n_sources]
        out_refs = refs[n_sources:-1]
        sems = refs[-1]
        tok_id = lax.axis_index("tok")
        copies = []
        for m in range(n_tok):
            start = m * head_size
            if mirrored:
                start = pl.multiple_of((tok_id ^ m) * head_size, head_size)
            for j in range(n_sources):
                columns = pl.ds(start, head_size)
                source = source_refs[j]
                view = source.at[:, :, columns] if len(shape) == 3 else source.at[:, columns]
                target = out_refs[m] if mirrored else out_refs[0].at[m]
                if n_sources > 1:
                    target = target.at[:, j * head_size : (j + 1) * head_size]
                copies.append(pltpu.make_async_copy(view, target, sems.at[m, j]))
                copies[-1].start()
        for copy in copies:
            copy.wait()

    if mirrored:
        out_shape = [jax.ShapeDtypeStruct(shape, dtype)] * n_tok
    else:
        out_shape = jax.ShapeDtypeStruct((n_tok,) + shape, dtype)
    return kernel(
        body,
        sources,
        out_shape,
        [ANY] * n_sources,
        [ANY] * n_tok if mirrored else ANY,
        [pltpu.SemaphoreType.DMA((n_tok, n_sources))],
        4,
        0,
        4 * n_sources * sources[0].size,
    )


def pick_sides(pieces, tables, n_region, n_tok):
    whole = not isinstance(pieces, list)
    _, rows, head_size = pieces.shape[1:] if whole else pieces[0].shape
    dtype = pieces.dtype if whole else pieces[0].dtype

    def neighbours():
        region_id = lax.axis_index("region")
        upper = lax.rem(region_id + 1, n_region)
        lower = lax.rem(region_id + n_region - 1, n_region)
        return (0, upper), (1, lower)

    def body(block_ref, frame_ref, slot_ref, *refs):
        piece_refs = refs[: -4 if not whole else 1]
        up_ref, down_ref, places, sems = refs[-4:]
        tok_id = lax.axis_index("tok")
        copies = []
        for (entry, reader), out_ref in zip(neighbours(), (up_ref, down_ref)):
            for m in range(n_tok):
                query_block = reader * n_tok + (tok_id ^ m)
                slot = slot_ref[block_ref[entry, query_block]]
                source = lax.rem(slot, n_tok)
                frame = frame_ref[entry, query_block]
                if whole:
                    copies.append(
                        pltpu.make_async_copy(
                            piece_refs[0].at[source, frame], out_ref.at[m], sems.at[entry, m]
                        )
                    )
                    copies[-1].start()
                else:
                    places[0, source ^ tok_id] = m
                    places[1, source ^ tok_id] = frame
            if not whole:
                for m in range(n_tok):
                    copies.append(
                        pltpu.make_async_copy(
                            piece_refs[m].at[places[1, m]],
                            out_ref.at[places[0, m]],
                            sems.at[entry, m],
                        )
                    )
                    copies[-1].start()
        for copy in copies:
            copy.wait()

    side = jax.ShapeDtypeStruct((n_tok, rows, head_size), dtype)
    return kernel(
        body,
        tables + ((pieces,) if whole else tuple(pieces)),
        [side, side],
        [SMEM] * 3 + [ANY] * (1 if whole else n_tok),
        [ANY] * 2,
        [pltpu.SMEM((2, n_tok), jnp.int32), pltpu.SemaphoreType.DMA((2, n_tok))],
        4,
        0,
        8 * n_tok * rows * head_size,
    )


def project(token_blocks, weight_rows):
    n_tok = len(token_blocks)
    rows, width = token_blocks[0].shape
    depth, columns = weight_rows[0].shape
    dtype = token_blocks[0].dtype
    n_chunks = 2
    chunk = n_tok // n_chunks

    def body(*refs):
        token_refs = refs[:n_tok]
        weight_refs = refs[n_tok : 2 * n_tok]
        out_ref, held, whole, sems = refs[2 * n_tok :]
        tok_id = lax.axis_index("tok")
        weight_copies = []
        for m in range(n_tok):
            start = pl.multiple_of((tok_id ^ m) * depth, depth)
            target = whole.at[pl.ds(start, depth), :]
            weight_copies.append(pltpu.make_async_copy(weight_refs[m], target, sems.at[0, m]))
            weight_copies[-1].start()
        token_copies = []
        for m in range(n_tok):
            target = held.at[m * rows : (m + 1) * rows]
            token_copies.append(pltpu.make_async_copy(token_refs[m], target, sems.at[1, m]))
            token_copies[-1].start()
        for copy in weight_copies:
            copy.wait()
        for c in range(n_chunks):
            for m in range(c * chunk, (c + 1) * chunk):
                token_copies[m].wait()
            some = slice(c * chunk * rows, (c + 1) * chunk * rows)
            out_ref[some] = jnp.dot(
                held[some], whole[...], preferred_element_type=jnp.float32
            ).astype(dtype)

    out = kernel(
        body,
        (*token_blocks, *weight_rows),
        jax.ShapeDtypeStruct((n_tok * rows, columns), dtype),
        [ANY] * (2 * n_tok),
        VMEM,
        [
            pltpu.VMEM((n_tok * rows, width), dtype),
            pltpu.VMEM((n_tok * depth, columns), dtype),
            pltpu.SemaphoreType.DMA((2, n_tok)),
        ],
        12,
        2 * n_tok * rows * width * columns,
        2 * n_tok * (rows * width + depth * columns),
    )
    return out.reshape(n_tok, rows, columns)


def attend(projected, keys, values, side_keys, side_values, tables, counts):
    n_tok, rows, columns = projected.shape
    head_size = columns // 3
    frames = keys.shape[1]
    max_entries = tables[0].shape[0]
    scale = head_size ** (-0.5)
    across = (((1,), (1,)), ((), ()))

    def body(block_ref, frame_ref, slot_ref, count_ref, proj_ref, key_ref, value_ref, *refs):
        side_refs = refs[:4]
        out_refs = refs[4:]
        region_id = lax.axis_index("region")
        tok_id = lax.axis_index("tok")
        for m in range(n_tok):
            query_block = region_id * n_tok + (tok_id ^ m)
            live = count_ref[query_block]
            query = proj_ref[m, :, :head_size]
            key_list = [proj_ref[m, :, head_size : 2 * head_size]]
            value_list = [proj_ref[m, :, 2 * head_size :]]
            for entry in range(2):
                key_list.append(side_refs[entry][m])
                value_list.append(side_refs[2 + entry][m])
            for entry in range(2, max_entries):
                slot = slot_ref[block_ref[entry, query_block]]
                source = lax.rem(slot, n_tok)
                frame = frame_ref[entry, query_block]
                key_list.append(key_ref[source ^ tok_id, frame])
                value_list.append(value_ref[source, frame])
            scores = (
                lax.dot_general(
                    query,
                    jnp.concatenate(key_list, 0),
                    across,
                    preferred_element_type=jnp.float32,
                )
                * scale
            )
            column = lax.broadcasted_iota(jnp.int32, scores.shape, 1)
            scores = jnp.where(column < (live + 1) * rows, scores, jnp.float32(-1e30))
            row_max = jnp.max(scores, axis=1, keepdims=True)
            weights = jnp.exp(scores - row_max)
            total = jnp.sum(weights, axis=1, keepdims=True)
            context = jnp.dot(
                weights.astype(jnp.bfloat16),
                jnp.concatenate(value_list, 0),
                preferred_element_type=jnp.float32,
            )
            out_refs[m][...] = (context / total).astype(out_refs[m].dtype)

    dtype = projected.dtype
    return kernel(
        body,
        (*tables, counts, projected, keys, values, *side_keys, *side_values),
        [jax.ShapeDtypeStruct((rows, head_size), dtype)] * n_tok,
        [SMEM] * 4 + [VMEM] * 7,
        [VMEM] * n_tok,
        [],
        16,
        4 * n_tok * rows * rows * (max_entries + 1) * head_size,
        4 * n_tok * frames * rows * head_size,
    )


def join(pieces):
    n_pieces = len(pieces)
    piece = pieces[0]

    def body(*refs):
        copies = [
            pltpu.make_async_copy(refs[m], refs[n_pieces].at[m], refs[-1].at[m])
            for m in range(n_pieces)
        ]
        for copy in copies:
            copy.start()
        for copy in copies:
            copy.wait()

    return kernel(
        body,
        tuple(pieces),
        jax.ShapeDtypeStruct((n_pieces,) + piece.shape, piece.dtype),
        [ANY] * n_pieces,
        ANY,
        [pltpu.SemaphoreType.DMA((n_pieces,))],
        4,
        0,
        4 * n_pieces * piece.size,
    )


def mix(context_heads, out_columns):
    n_tok = len(context_heads)
    rows, head_size = context_heads[0].shape
    width, columns = out_columns[0].shape
    dtype = context_heads[0].dtype

    def body(*refs):
        context_refs = refs[:n_tok]
        column_refs = refs[n_tok : 2 * n_tok]
        out_ref, context, held, sems = refs[2 * n_tok :]
        copies = [
            pltpu.make_async_copy(
                column_refs[m],
                held.at[m // 2, :, m % 2 * columns : (m % 2 + 1) * columns],
                sems.at[m],
            )
            for m in range(n_tok)
        ]
        for copy in copies:
            copy.start()
        tok_id = lax.axis_index("tok")
        for m in range(n_tok):
            start = pl.multiple_of((tok_id ^ m) * head_size, head_size)
            context[:, pl.ds(start, head_size)] = context_refs[m][...]
        for m in range(0, n_tok, 2):
            copies[m].wait()
            copies[m + 1].wait()
            mixed = jnp.dot(context[...], held[m // 2], preferred_element_type=jnp.float32)
            for j in range(2):
                start = pl.multiple_of((tok_id ^ (m + j)) * columns, columns)
                out_ref[:, pl.ds(start, columns)] = mixed[
                    :, j * columns : (j + 1) * columns
                ].astype(dtype)

    return kernel(
        body,
        (*context_heads, *out_columns),
        jax.ShapeDtypeStruct((rows, n_tok * columns), dtype),
        [VMEM] * n_tok + [ANY] * n_tok,
        VMEM,
        [
            pltpu.VMEM((rows, n_tok * head_size), dtype),
            pltpu.VMEM((n_tok // 2, width, 2 * columns), dtype),
            pltpu.SemaphoreType.DMA((n_tok,)),
        ],
        12,
        2 * rows * width * n_tok * columns,
        2 * width * n_tok * columns,
    )


def head_per_device(
    tokens,
    w_query,
    w_key,
    w_value,
    w_out,
    past_keys,
    past_values,
    nb_block,
    nb_frame,
    nb_count,
    block_slot,
):
    n_region = lax.axis_size("region")
    n_tok = lax.axis_size("tok")
    tables = (nb_block.T, nb_frame.T, block_slot)
    keys = exchanged(pack((past_keys,), n_tok, True))
    values = swapped(pack((past_values,), n_tok, False))
    up_keys, down_keys = pick_sides(keys, tables, n_region, n_tok)
    below_keys = shifted(up_keys, "region", 1)
    above_keys = shifted(down_keys, "region", -1)
    up_values, down_values = pick_sides(values, tables, n_region, n_tok)
    below_values = shifted(up_values, "region", 1)
    above_values = shifted(down_values, "region", -1)
    weight_rows = exchanged(pack((w_query, w_key, w_value), n_tok, True))
    token_blocks = gathered(tokens)
    out_columns = gathered(w_out)
    projected = project(token_blocks, weight_rows)
    context = attend(
        projected,
        join(keys),
        values,
        (below_keys, above_keys),
        (below_values, above_values),
        tables,
        nb_count,
    )
    return mix(exchanged(context), out_columns)


def per_device(
    tokens,
    w_query,
    w_key,
    w_value,
    w_out,
    past_keys,
    past_values,
    nb_block,
    nb_frame,
    nb_count,
    block_slot,
):
    n_region = lax.axis_size("region")
    n_tok = lax.axis_size("tok")
    region_id = lax.axis_index("region")
    tok_id = lax.axis_index("tok")
    n_devices = n_region * n_tok
    my_device = region_id * n_tok + tok_id
    tok_rows, model_width = tokens.shape
    blocks_dev = tok_rows // QB
    n_blocks, max_entries = nb_block.shape
    head_size = model_width // HEADS
    whole_query, whole_key, whole_value = (
        lax.all_gather(w_query, "tok", axis=0, tiled=True),
        lax.all_gather(w_key, "tok", axis=0, tiled=True),
        lax.all_gather(w_value, "tok", axis=0, tiled=True),
    )
    proj_query = jnp.dot(tokens, whole_query, preferred_element_type=jnp.float32)
    proj_key = jnp.dot(tokens, whole_key, preferred_element_type=jnp.float32)
    proj_value = jnp.dot(tokens, whole_value, preferred_element_type=jnp.float32)
    queries = proj_query.astype(jnp.bfloat16)
    keys_new = proj_key.astype(jnp.bfloat16)
    values_new = proj_value.astype(jnp.bfloat16)
    slot_table = jnp.take(block_slot, nb_block, axis=0)
    source_dev = slot_table // blocks_dev
    source_tok = source_dev % n_tok
    flat_table = nb_frame * blocks_dev + slot_table % blocks_dev
    live_table = jnp.arange(max_entries, dtype=jnp.int32)[None, :] < nb_count[:, None]
    dest_tok = jnp.arange(n_blocks, dtype=jnp.int32) // blocks_dev % n_tok
    tok_range = jnp.arange(n_tok, dtype=jnp.int32)
    mine_flat = (live_table & (source_dev == my_device)).reshape(-1)
    dest_flat = jnp.broadcast_to(dest_tok[:, None], (n_blocks, max_entries)).reshape(-1)
    matches = mine_flat[None, :] & (dest_flat[None, :] == tok_range[:, None])
    offer_index = jnp.max(jnp.where(matches, flat_table.reshape(-1)[None, :], 0), axis=1)
    offer_keys = jnp.take(past_keys, offer_index, axis=0)
    offer_values = jnp.take(past_values, offer_index, axis=0)
    lead_tok = source_tok.reshape(n_devices, blocks_dev, max_entries)[:, 0, :2]
    lower_region = (region_id + n_region - 1) % n_region
    upper_region = (region_id + 1) % n_region
    my_start = my_device * blocks_dev
    my_tok_table = lax.dynamic_slice_in_dim(source_tok, my_start, blocks_dev, 0)
    got_keys, got_values = (
        lax.all_to_all(offer_keys, "tok", split_axis=0, concat_axis=0, tiled=True),
        lax.all_to_all(offer_values, "tok", split_axis=0, concat_axis=0, tiled=True),
    )
    upward_index = lax.dynamic_index_in_dim(
        lead_tok[:, 0], upper_region * n_tok + tok_id, 0, keepdims=False
    )
    downward_index = lax.dynamic_index_in_dim(
        lead_tok[:, 1], lower_region * n_tok + tok_id, 0, keepdims=False
    )
    upward_pair = jnp.concatenate(
        [
            lax.dynamic_slice_in_dim(got_keys, upward_index, 1, 0),
            lax.dynamic_slice_in_dim(got_values, upward_index, 1, 0),
        ],
        0,
    )
    downward_pair = jnp.concatenate(
        [
            lax.dynamic_slice_in_dim(got_keys, downward_index, 1, 0),
            lax.dynamic_slice_in_dim(got_values, downward_index, 1, 0),
        ],
        0,
    )
    below_pair = shifted(upward_pair, "region", 1)
    above_pair = shifted(downward_pair, "region", -1)
    own_index = my_tok_table[:, 2:].reshape(-1)
    own_keys = jnp.take(got_keys, own_index, axis=0).reshape(
        blocks_dev, (max_entries - 2) * QB, model_width
    )
    own_values = jnp.take(got_values, own_index, axis=0).reshape(
        blocks_dev, (max_entries - 2) * QB, model_width
    )
    side_keys = jnp.concatenate([below_pair[0], above_pair[0]], 0)[None]
    side_values = jnp.concatenate([below_pair[1], above_pair[1]], 0)[None]
    far_keys = jnp.concatenate([side_keys, own_keys], 1)
    far_values = jnp.concatenate([side_values, own_values], 1)
    key_list = jnp.concatenate([keys_new.reshape(blocks_dev, QB, model_width), far_keys], 1)
    value_list = jnp.concatenate([values_new.reshape(blocks_dev, QB, model_width), far_values], 1)
    list_len = key_list.shape[1]
    query_heads = queries.reshape(blocks_dev, QB, HEADS, head_size)
    key_heads = key_list.reshape(blocks_dev, list_len, HEADS, head_size)
    value_heads = value_list.reshape(blocks_dev, list_len, HEADS, head_size)
    attn_scale = head_size ** (-0.5)
    scores = (
        jnp.einsum("bqhd,bkhd->bhqk", query_heads, key_heads, preferred_element_type=jnp.float32)
        * attn_scale
    )
    my_counts = lax.dynamic_slice_in_dim(nb_count, my_start, blocks_dev, 0)
    entry_live = jnp.arange(max_entries, dtype=jnp.int32)[None, :] < my_counts[:, None]
    live_mask = jnp.concatenate(
        [jnp.ones((blocks_dev, QB), bool), jnp.repeat(entry_live, QB, axis=1)], 1
    )
    scores = jnp.where(live_mask[:, None, None, :], scores, jnp.float32(-1e30))
    row_max = jnp.max(scores, axis=-1, keepdims=True)
    exp_weights = jnp.where(
        live_mask[:, None, None, :], jnp.exp(scores - row_max), jnp.float32(0.0)
    )
    row_total = jnp.sum(exp_weights, axis=-1)
    prob_bf = exp_weights.astype(jnp.bfloat16)
    context = jnp.einsum(
        "bhqk,bkhd->bqhd", prob_bf, value_heads, preferred_element_type=jnp.float32
    )
    context = context / jnp.swapaxes(row_total, 1, 2)[:, :, :, None]
    context_bf = context.reshape(tok_rows, model_width).astype(jnp.bfloat16)
    whole_out = lax.all_gather(w_out, "tok", axis=1, tiled=True)
    mixed_out = jnp.dot(context_bf, whole_out, preferred_element_type=jnp.float32)
    return mixed_out.astype(jnp.bfloat16)


def solution(mesh):
    by_head = mesh.shape["tok"] == HEADS
    return jax.shard_map(
        head_per_device if by_head else per_device,
        mesh=mesh,
        in_specs=(
            P(("region", "tok"), None),
            P("tok", None),
            P("tok", None),
            P("tok", None),
            P(None, "tok"),
            P(None, ("region", "tok"), None),
            P(None, ("region", "tok"), None),
            P(),
            P(),
            P(),
            P(),
        ),
        out_specs=P(("region", "tok"), None),
        check_vma=False,
    )
```

```python
import math

import jax
import jax.numpy as jnp
from jax import lax
from jax.experimental import pallas as pl
from jax.experimental.pallas import tpu as pltpu
from jax.sharding import PartitionSpec as P

HEADS = 8
QB = 128


ANY = pl.BlockSpec(memory_space=pl.ANY)
VMEM = pl.BlockSpec(memory_space=pltpu.VMEM)
SMEM = pl.BlockSpec(memory_space=pltpu.SMEM)


def shifted(block, axis, distance):
    devices = range(lax.axis_size(axis))
    route = [((i - distance) % len(devices), i) for i in devices]
    return lax.ppermute(block, axis, route)


def partner(block, mask):
    route = [(i, i ^ mask) for i in range(lax.axis_size("tok"))]
    return lax.ppermute(block, "tok", route)


def gathered(shard):
    shards = [shard]
    for mask in range(1, lax.axis_size("tok")):
        near = mask % 2 == 1
        shards.append(partner(shards[mask - 1] if near else shard, 1 if near else mask))
    return shards


def exchanged(pieces):
    return [pieces[0]] + [partner(pieces[m], m) for m in range(1, len(pieces))]


def kernel(body, arguments, out_shape, in_specs, out_specs, scratch, limit, flops, moved):
    return pl.pallas_call(
        body,
        out_shape=out_shape,
        in_specs=in_specs,
        out_specs=out_specs,
        scratch_shapes=scratch,
        compiler_params=pltpu.CompilerParams(vmem_limit_bytes=limit * 2**20),
        cost_estimate=pl.CostEstimate(flops=flops, bytes_accessed=moved, transcendentals=0),
    )(*arguments)


def pack(sources, n_tok, mirrored):
    width = sources[0].shape[-1]
    head_size = width // n_tok
    n_sources = len(sources)
    shape = sources[0].shape[:-1] + (n_sources * head_size,)
    dtype = sources[0].dtype

    def body(*refs):
        source_refs = refs[:n_sources]
        out_refs = refs[n_sources:-1]
        sems = refs[-1]
        tok_id = lax.axis_index("tok")
        copies = []
        for m in range(n_tok):
            start = m * head_size
            if mirrored:
                start = pl.multiple_of((tok_id ^ m) * head_size, head_size)
            for j in range(n_sources):
                columns = pl.ds(start, head_size)
                source = source_refs[j]
                view = source.at[:, :, columns] if len(shape) == 3 else source.at[:, columns]
                target = out_refs[m] if mirrored else out_refs[0].at[m]
                if n_sources > 1:
                    target = target.at[:, j * head_size : (j + 1) * head_size]
                copies.append(pltpu.make_async_copy(view, target, sems.at[m, j]))
                copies[-1].start()
        for copy in copies:
            copy.wait()

    if mirrored:
        out_shape = [jax.ShapeDtypeStruct(shape, dtype)] * n_tok
    else:
        out_shape = jax.ShapeDtypeStruct((n_tok,) + shape, dtype)
    return kernel(
        body,
        sources,
        out_shape,
        [ANY] * n_sources,
        [ANY] * n_tok if mirrored else ANY,
        [pltpu.SemaphoreType.DMA((n_tok, n_sources))],
        4,
        0,
        4 * n_sources * sources[0].size,
    )


def cached_at(list_ref, entry, query_block, n_tok):
    max_entries = list_ref.shape[0] // 2 - 1
    slot = list_ref[2 * max_entries + 1, list_ref[entry, query_block]]
    return lax.rem(slot, n_tok), list_ref[max_entries + entry, query_block]


def pick_sides(pieces, lists, n_region, n_tok):
    whole = not isinstance(pieces, list)
    _, rows, head_size = pieces.shape[1:] if whole else pieces[0].shape
    dtype = pieces.dtype if whole else pieces[0].dtype

    def neighbours():
        region_id = lax.axis_index("region")
        upper = lax.rem(region_id + 1, n_region)
        lower = lax.rem(region_id + n_region - 1, n_region)
        return (0, upper), (1, lower)

    def body(list_ref, *refs):
        piece_refs = refs[: -4 if not whole else 1]
        up_ref, down_ref, places, sems = refs[-4:]
        tok_id = lax.axis_index("tok")
        copies = []
        for (entry, reader), out_ref in zip(neighbours(), (up_ref, down_ref)):
            for m in range(n_tok):
                query_block = reader * n_tok + (tok_id ^ m)
                source, frame = cached_at(list_ref, entry, query_block, n_tok)
                if whole:
                    copies.append(
                        pltpu.make_async_copy(
                            piece_refs[0].at[source, frame], out_ref.at[m], sems.at[entry, m]
                        )
                    )
                    copies[-1].start()
                else:
                    places[0, source ^ tok_id] = m
                    places[1, source ^ tok_id] = frame
            if not whole:
                for m in range(n_tok):
                    copies.append(
                        pltpu.make_async_copy(
                            piece_refs[m].at[places[1, m]],
                            out_ref.at[places[0, m]],
                            sems.at[entry, m],
                        )
                    )
                    copies[-1].start()
        for copy in copies:
            copy.wait()

    side = jax.ShapeDtypeStruct((n_tok, rows, head_size), dtype)
    return kernel(
        body,
        (lists, pieces) if whole else (lists, *pieces),
        [side, side],
        [SMEM] + [ANY] * (1 if whole else n_tok),
        [ANY] * 2,
        [pltpu.SMEM((2, n_tok), jnp.int32), pltpu.SemaphoreType.DMA((2, n_tok))],
        4,
        0,
        8 * n_tok * rows * head_size,
    )


def project(token_blocks, weight_rows):
    n_tok = len(token_blocks)
    rows, width = token_blocks[0].shape
    depth, columns = weight_rows[0].shape
    dtype = token_blocks[0].dtype

    def body(*refs):
        token_refs = refs[:n_tok]
        weight_refs = refs[n_tok : 2 * n_tok]
        out_ref, whole = refs[2 * n_tok :]
        tok_id = lax.axis_index("tok")
        for m in range(n_tok):
            start = pl.multiple_of((tok_id ^ m) * depth, depth)
            whole[pl.ds(start, depth), :] = weight_refs[m][...]
        tokens = jnp.concatenate([ref[...] for ref in token_refs], 0)
        out_ref[...] = jnp.dot(
            tokens, whole[...], preferred_element_type=jnp.float32
        ).astype(dtype)

    out = kernel(
        body,
        (*token_blocks, *weight_rows),
        jax.ShapeDtypeStruct((n_tok * rows, columns), dtype),
        [VMEM] * (2 * n_tok),
        VMEM,
        [pltpu.VMEM((n_tok * depth, columns), dtype)],
        14,
        2 * n_tok * rows * width * columns,
        2 * n_tok * (rows * width + depth * columns),
    )
    return out.reshape(n_tok, rows, columns)


def attend(projected, keys, values, side_keys, side_values, lists):
    n_tok, rows, columns = projected.shape
    head_size = columns // 3
    frames = values.shape[1]
    max_entries = lists.shape[0] // 2 - 1
    length = (max_entries + 1) * rows
    base = head_size ** (-0.5) * math.log2(math.e)
    across = (((1,), (1,)), ((), ()))
    chunk = 32
    always = 3

    def body(list_ref, proj_ref, key_ref, value_ref, *refs):
        side_refs = refs[:4]
        out_refs = refs[4 : 4 + n_tok]
        score_ref, prob_ref = refs[4 + n_tok :]
        region_id = lax.axis_index("region")
        tok_id = lax.axis_index("tok")

        def listed(m, own, sides, cached_ref):
            query_block = region_id * n_tok + (tok_id ^ m)
            found = [own] + [side[m] for side in sides]
            for entry in range(2, max_entries):
                source, frame = cached_at(list_ref, entry, query_block, n_tok)
                found.append(cached_ref[source ^ tok_id, frame])
            return jnp.concatenate(found, 0)

        def score(m):
            score_ref[m % 2] = lax.dot_general(
                proj_ref[m, :, :head_size],
                listed(m, proj_ref[m, :, head_size : 2 * head_size], side_refs[:2], key_ref),
                across,
                preferred_element_type=jnp.float32,
            )

        def soften(m):
            live = list_ref[2 * max_entries, region_id * n_tok + (tok_id ^ m)]
            totals = []
            for row in range(0, rows, chunk):
                some = slice(row, row + chunk)
                blocks = [score_ref[m % 2, some, : always * rows]]
                for entry in range(always - 1, max_entries):
                    block = score_ref[m % 2, some, (entry + 1) * rows : (entry + 2) * rows]
                    blocks.append(jnp.where(entry < live, block, jnp.float32(-1e30)))
                scores = jnp.concatenate(blocks, 1)
                row_max = jnp.max(scores, axis=1, keepdims=True)
                weights = jnp.exp2((scores - row_max) * base)
                totals.append(jnp.sum(weights, axis=1, keepdims=True))
                prob_ref[m % 2, some] = weights.astype(jnp.bfloat16)
            return jnp.concatenate(totals, 0)

        score(0)
        for m in range(n_tok):
            if m + 1 < n_tok:
                score(m + 1)
            total = soften(m)
            context = jnp.dot(
                prob_ref[m % 2],
                listed(m, proj_ref[m, :, 2 * head_size :], side_refs[2:], value_ref),
                preferred_element_type=jnp.float32,
            )
            out_refs[m][...] = (context / total).astype(out_refs[m].dtype)

    dtype = projected.dtype
    return kernel(
        body,
        (lists, projected, keys, values, *side_keys, *side_values),
        [jax.ShapeDtypeStruct((rows, head_size), dtype)] * n_tok,
        [SMEM] + [VMEM] * 7,
        [VMEM] * n_tok,
        [
            pltpu.VMEM((2, rows, length), jnp.float32),
            pltpu.VMEM((2, rows, length), dtype),
        ],
        16,
        4 * n_tok * rows * length * head_size,
        4 * n_tok * frames * rows * head_size,
    )


def join(pieces):
    n_pieces = len(pieces)
    piece = pieces[0]

    def body(*refs):
        copies = [
            pltpu.make_async_copy(refs[m], refs[n_pieces].at[m], refs[-1].at[m])
            for m in range(n_pieces)
        ]
        for copy in copies:
            copy.start()
        for copy in copies:
            copy.wait()

    return kernel(
        body,
        tuple(pieces),
        jax.ShapeDtypeStruct((n_pieces,) + piece.shape, piece.dtype),
        [ANY] * n_pieces,
        VMEM,
        [pltpu.SemaphoreType.DMA((n_pieces,))],
        4,
        0,
        4 * n_pieces * piece.size,
    )


def mix(context_heads, out_columns):
    n_tok = len(context_heads)
    rows, head_size = context_heads[0].shape
    width, columns = out_columns[0].shape
    dtype = context_heads[0].dtype

    def body(*refs):
        context_refs = refs[:n_tok]
        column_refs = refs[n_tok : 2 * n_tok]
        out_ref, context = refs[2 * n_tok :]
        tok_id = lax.axis_index("tok")
        for m in range(n_tok):
            start = pl.multiple_of((tok_id ^ m) * head_size, head_size)
            context[:, pl.ds(start, head_size)] = context_refs[m][...]
        for m in range(0, n_tok, 2):
            pair = jnp.concatenate([column_refs[m][...], column_refs[m + 1][...]], 1)
            mixed = jnp.dot(context[...], pair, preferred_element_type=jnp.float32)
            for j in range(2):
                start = pl.multiple_of((tok_id ^ (m + j)) * columns, columns)
                out_ref[:, pl.ds(start, columns)] = mixed[
                    :, j * columns : (j + 1) * columns
                ].astype(dtype)

    return kernel(
        body,
        (*context_heads, *out_columns),
        jax.ShapeDtypeStruct((rows, n_tok * columns), dtype),
        [VMEM] * (2 * n_tok),
        VMEM,
        [pltpu.VMEM((rows, n_tok * head_size), dtype)],
        12,
        2 * rows * width * n_tok * columns,
        2 * width * n_tok * columns,
    )


def head_per_device(
    tokens,
    w_query,
    w_key,
    w_value,
    w_out,
    past_keys,
    past_values,
    nb_block,
    nb_frame,
    nb_count,
    block_slot,
):
    n_region = lax.axis_size("region")
    n_tok = lax.axis_size("tok")
    lists = jnp.concatenate(
        [nb_block.T, nb_frame.T, nb_count[None], block_slot[None]], 0
    )
    keys = exchanged(pack((past_keys,), n_tok, True))
    values = exchanged(pack((past_values,), n_tok, True))
    up_keys, down_keys = pick_sides(keys, lists, n_region, n_tok)
    below_keys = shifted(up_keys, "region", 1)
    above_keys = shifted(down_keys, "region", -1)
    up_values, down_values = pick_sides(values, lists, n_region, n_tok)
    below_values = shifted(up_values, "region", 1)
    above_values = shifted(down_values, "region", -1)
    weight_rows = exchanged(pack((w_query, w_key, w_value), n_tok, True))
    token_blocks = gathered(tokens)
    out_columns = gathered(w_out)
    projected = project(token_blocks, weight_rows)
    context = attend(
        projected,
        join(keys),
        join(values),
        (below_keys, above_keys),
        (below_values, above_values),
        lists,
    )
    return mix(exchanged(context), out_columns)


def per_device(
    tokens,
    w_query,
    w_key,
    w_value,
    w_out,
    past_keys,
    past_values,
    nb_block,
    nb_frame,
    nb_count,
    block_slot,
):
    n_region = lax.axis_size("region")
    n_tok = lax.axis_size("tok")
    region_id = lax.axis_index("region")
    tok_id = lax.axis_index("tok")
    n_devices = n_region * n_tok
    my_device = region_id * n_tok + tok_id
    tok_rows, model_width = tokens.shape
    blocks_dev = tok_rows // QB
    n_blocks, max_entries = nb_block.shape
    head_size = model_width // HEADS
    whole_query, whole_key, whole_value = (
        lax.all_gather(w_query, "tok", axis=0, tiled=True),
        lax.all_gather(w_key, "tok", axis=0, tiled=True),
        lax.all_gather(w_value, "tok", axis=0, tiled=True),
    )
    proj_query = jnp.dot(tokens, whole_query, preferred_element_type=jnp.float32)
    proj_key = jnp.dot(tokens, whole_key, preferred_element_type=jnp.float32)
    proj_value = jnp.dot(tokens, whole_value, preferred_element_type=jnp.float32)
    queries = proj_query.astype(jnp.bfloat16)
    keys_new = proj_key.astype(jnp.bfloat16)
    values_new = proj_value.astype(jnp.bfloat16)
    slot_table = jnp.take(block_slot, nb_block, axis=0)
    source_dev = slot_table // blocks_dev
    source_tok = source_dev % n_tok
    flat_table = nb_frame * blocks_dev + slot_table % blocks_dev
    live_table = jnp.arange(max_entries, dtype=jnp.int32)[None, :] < nb_count[:, None]
    dest_tok = jnp.arange(n_blocks, dtype=jnp.int32) // blocks_dev % n_tok
    tok_range = jnp.arange(n_tok, dtype=jnp.int32)
    mine_flat = (live_table & (source_dev == my_device)).reshape(-1)
    dest_flat = jnp.broadcast_to(dest_tok[:, None], (n_blocks, max_entries)).reshape(-1)
    matches = mine_flat[None, :] & (dest_flat[None, :] == tok_range[:, None])
    offer_index = jnp.max(jnp.where(matches, flat_table.reshape(-1)[None, :], 0), axis=1)
    offer_keys = jnp.take(past_keys, offer_index, axis=0)
    offer_values = jnp.take(past_values, offer_index, axis=0)
    lead_tok = source_tok.reshape(n_devices, blocks_dev, max_entries)[:, 0, :2]
    lower_region = (region_id + n_region - 1) % n_region
    upper_region = (region_id + 1) % n_region
    my_start = my_device * blocks_dev
    my_tok_table = lax.dynamic_slice_in_dim(source_tok, my_start, blocks_dev, 0)
    got_keys, got_values = (
        lax.all_to_all(offer_keys, "tok", split_axis=0, concat_axis=0, tiled=True),
        lax.all_to_all(offer_values, "tok", split_axis=0, concat_axis=0, tiled=True),
    )
    upward_index = lax.dynamic_index_in_dim(
        lead_tok[:, 0], upper_region * n_tok + tok_id, 0, keepdims=False
    )
    downward_index = lax.dynamic_index_in_dim(
        lead_tok[:, 1], lower_region * n_tok + tok_id, 0, keepdims=False
    )
    upward_pair = jnp.concatenate(
        [
            lax.dynamic_slice_in_dim(got_keys, upward_index, 1, 0),
            lax.dynamic_slice_in_dim(got_values, upward_index, 1, 0),
        ],
        0,
    )
    downward_pair = jnp.concatenate(
        [
            lax.dynamic_slice_in_dim(got_keys, downward_index, 1, 0),
            lax.dynamic_slice_in_dim(got_values, downward_index, 1, 0),
        ],
        0,
    )
    below_pair = shifted(upward_pair, "region", 1)
    above_pair = shifted(downward_pair, "region", -1)
    own_index = my_tok_table[:, 2:].reshape(-1)
    own_keys = jnp.take(got_keys, own_index, axis=0).reshape(
        blocks_dev, (max_entries - 2) * QB, model_width
    )
    own_values = jnp.take(got_values, own_index, axis=0).reshape(
        blocks_dev, (max_entries - 2) * QB, model_width
    )
    side_keys = jnp.concatenate([below_pair[0], above_pair[0]], 0)[None]
    side_values = jnp.concatenate([below_pair[1], above_pair[1]], 0)[None]
    far_keys = jnp.concatenate([side_keys, own_keys], 1)
    far_values = jnp.concatenate([side_values, own_values], 1)
    key_list = jnp.concatenate([keys_new.reshape(blocks_dev, QB, model_width), far_keys], 1)
    value_list = jnp.concatenate([values_new.reshape(blocks_dev, QB, model_width), far_values], 1)
    list_len = key_list.shape[1]
    query_heads = queries.reshape(blocks_dev, QB, HEADS, head_size)
    key_heads = key_list.reshape(blocks_dev, list_len, HEADS, head_size)
    value_heads = value_list.reshape(blocks_dev, list_len, HEADS, head_size)
    attn_scale = head_size ** (-0.5)
    scores = (
        jnp.einsum("bqhd,bkhd->bhqk", query_heads, key_heads, preferred_element_type=jnp.float32)
        * attn_scale
    )
    my_counts = lax.dynamic_slice_in_dim(nb_count, my_start, blocks_dev, 0)
    entry_live = jnp.arange(max_entries, dtype=jnp.int32)[None, :] < my_counts[:, None]
    live_mask = jnp.concatenate(
        [jnp.ones((blocks_dev, QB), bool), jnp.repeat(entry_live, QB, axis=1)], 1
    )
    scores = jnp.where(live_mask[:, None, None, :], scores, jnp.float32(-1e30))
    row_max = jnp.max(scores, axis=-1, keepdims=True)
    exp_weights = jnp.where(
        live_mask[:, None, None, :], jnp.exp(scores - row_max), jnp.float32(0.0)
    )
    row_total = jnp.sum(exp_weights, axis=-1)
    prob_bf = exp_weights.astype(jnp.bfloat16)
    context = jnp.einsum(
        "bhqk,bkhd->bqhd", prob_bf, value_heads, preferred_element_type=jnp.float32
    )
    context = context / jnp.swapaxes(row_total, 1, 2)[:, :, :, None]
    context_bf = context.reshape(tok_rows, model_width).astype(jnp.bfloat16)
    whole_out = lax.all_gather(w_out, "tok", axis=1, tiled=True)
    mixed_out = jnp.dot(context_bf, whole_out, preferred_element_type=jnp.float32)
    return mixed_out.astype(jnp.bfloat16)


def solution(mesh):
    by_head = mesh.shape["tok"] == HEADS
    return jax.shard_map(
        head_per_device if by_head else per_device,
        mesh=mesh,
        in_specs=(
            P(("region", "tok"), None),
            P("tok", None),
            P("tok", None),
            P("tok", None),
            P(None, "tok"),
            P(None, ("region", "tok"), None),
            P(None, ("region", "tok"), None),
            P(),
            P(),
            P(),
            P(),
        ),
        out_specs=P(("region", "tok"), None),
        check_vma=False,
    )
```
